32 devices in a mesh: strike: 16 (over z, y, core), depth: 2 (over x).
Axes of the slice: x: 2, y: 2, z: 4, core: 2. Of those that a mesh axis runs over, the one named last changes fastest.
Arguments:
- velocity: float32 [3, 16, 32, 2048], P(None, 'depth', None, 'strike'), may hold values from -6 to 6
- stress: float32 [6, 16, 32, 2048], P(None, 'depth', None, 'strike'), may hold values from -6 to 6
- buoyancy: float32 [16, 32, 2048], P('depth', None, 'strike'), may hold values from 0.5 to 1
- lame_lambda: float32 [16, 32, 2048], P('depth', None, 'strike'), may hold values from 0.3 to 0.8
- shear_modulus: float32 [16, 32, 2048], P('depth', None, 'strike'), may hold values from 0.3 to 0.8
- past_rates: float32 [64, 16, 2048], P(None, 'depth', 'strike'), may hold values from -6 to 6
- memory_coefs: float32 [64], replicated, may hold values from 0.02 to 0.2
- prestress: float32 [16, 2048], P('depth', 'strike'), may hold values from -6 to 6
- fault_mask: int32 [16, 2048], P('depth', 'strike'), may hold values 0 or 1
Outputs:
- velocity_out: float32 [3, 16, 32, 2048], P(None, 'depth', None, 'strike')
- stress_out: float32 [6, 16, 32, 2048], P(None, 'depth', None, 'strike')
The draws below stay inside these ranges and needn't reach their ends.
All inputs are finite; a program needn't handle non-finite values. No bound on the sum of `fault_mask` on one device may be relied on, other than what follows from the above.
Results may differ from the reference program's by a relative error of at most 0.0001.
Values sent between devices are 32-bit elements; how exact they have to be, the bound alone decides.
A program may use at most 64 MiB of HBM per device.

```python
import math
import jax
import jax.numpy as jnp
from jax import lax

CX = 128
NY = 32
HIST = 64
STEPS = 8
NX = 2048
NZ = 16


def with_ends(entries, rng, smallest, top_value):
    shape = entries.shape
    place = [jax.random.randint(jax.random.fold_in(rng, axis), (), 0, shape[axis]) for axis in range(len(shape))]
    entries = entries.at[tuple(place)].set(smallest)
    longest = shape.index(max(shape))
    place[longest] = (place[longest] + 1) % shape[longest]
    return entries.at[tuple(place)].set(top_value)


def block_scale(rng, shape, split, smallest, largest):
    loudness = 1.0
    for dim, parts in split:
        steps = jax.random.uniform(jax.random.fold_in(jax.random.fold_in(rng, 6), dim), (parts,), jnp.float32, smallest / len(split), largest / len(split))
        loudness = loudness * jnp.repeat(jnp.exp(steps), shape[dim] // parts).reshape((-1,) + (1,) * (len(shape) - 1 - dim))
    return loudness


def noise(rng, shape, deviation, reach, shards=(), dtype=jnp.bfloat16):
    loudness = block_scale(rng, shape, shards, -0.22, 0.18) if shards else 1.0
    result = jax.random.normal(rng, shape, jnp.float32) * deviation * loudness
    return jnp.minimum(jnp.maximum(result, -reach), reach).astype(dtype)


def setup_inputs(seed: int = 0) -> dict:
    key_of = jax.random.split(jax.random.key(seed), 10)
    return {
        "velocity": noise(key_of[0], (3, NZ, NY, NX), 1.0, 6.0, ((1, 2), (3, 16)), jnp.float32),
        "stress": noise(key_of[1], (6, NZ, NY, NX), 1.0, 6.0, ((1, 2), (3, 16)), jnp.float32),
        "buoyancy": jnp.clip(jnp.exp(math.log(1.0) - 0.6931472 * jax.random.uniform(key_of[2], (NZ, NY, NX), jnp.float32) ** block_scale(key_of[2], (NZ, NY, NX), ((0, 2), (2, 16)), -0.2, 0.2)), 0.5, 1.0),
        "lame_lambda": jnp.clip(jnp.exp(math.log(0.8) - 0.98082923 * jax.random.uniform(key_of[3], (NZ, NY, NX), jnp.float32) ** block_scale(key_of[3], (NZ, NY, NX), ((0, 2), (2, 16)), -0.2, 0.2)), 0.3, 0.8),
        "shear_modulus": jnp.clip(jnp.exp(math.log(0.8) - 0.98082923 * jax.random.uniform(key_of[4], (NZ, NY, NX), jnp.float32) ** block_scale(key_of[4], (NZ, NY, NX), ((0, 2), (2, 16)), -0.2, 0.2)), 0.3, 0.8),
        "past_rates": noise(key_of[5], (HIST, NZ, NX), 1.0, 6.0, ((1, 2), (2, 16)), jnp.float32),
        "memory_coefs": jnp.clip(jnp.exp(jax.random.uniform(key_of[6], (HIST,), jnp.float32, math.log(0.02), math.log(0.2))), 0.02, 0.2),
        "prestress": noise(key_of[7], (NZ, NX), 1.0, 6.0, ((0, 2), (1, 16)), jnp.float32),
        "fault_mask": with_ends((jax.random.randint(key_of[8], (NZ, NX), 0, 4) < 3).astype(jnp.int32), jax.random.fold_in(key_of[8], 1), 0, 1),
    }


DT = 0.3
FRIC = 0.5


def ahead_x(f):
    return jnp.roll(f, -1, 2)


def behind_x(f):
    return jnp.roll(f, 1, 2)


def ahead_y(f):
    return jnp.concatenate([f[:, 1:], jnp.zeros_like(f[:, :1])], axis=1)


def behind_y(f):
    return jnp.concatenate([jnp.zeros_like(f[:, :1]), f[:, :-1]], axis=1)


def ahead_z(f):
    return jnp.concatenate([f[1:], jnp.zeros_like(f[:1])], axis=0)


def behind_z(f):
    return jnp.concatenate([jnp.zeros_like(f[:1]), f[:-1]], axis=0)


def reference(velocity, stress, buoyancy, lame_lambda, shear_modulus, past_rates, memory_coefs, prestress, fault_mask):
    vx, vy, vz = velocity[0], velocity[1], velocity[2]
    sxx, sxy, sxz, syz, szz, syy = stress[0], stress[1], stress[2], stress[3], stress[4], stress[5]
    center = vx.shape[1] // 2
    stiff = lame_lambda + 2.0 * shear_modulus
    history = past_rates
    for step in range(STEPS):
        vx = vx + DT * buoyancy * ((ahead_x(sxx) - sxx) + (sxy - behind_y(sxy)) + (sxz - behind_z(sxz)))
        vy = vy + DT * buoyancy * ((sxy - behind_x(sxy)) + (ahead_y(syy) - syy) + (syz - behind_z(syz)))
        vz = vz + DT * buoyancy * ((sxz - behind_x(sxz)) + (syz - behind_y(syz)) + (ahead_z(szz) - szz))
        rate = vx[:, center + 1, :] - vx[:, center, :]
        memory = jnp.tensordot(memory_coefs, history, axes=1, precision=lax.Precision.HIGHEST)
        strain_x = vx - behind_x(vx)
        strain_y = vy - behind_y(vy)
        strain_z = vz - behind_z(vz)
        sxx = sxx + DT * (stiff * strain_x + lame_lambda * (strain_y + strain_z))
        syy = syy + DT * (stiff * strain_y + lame_lambda * (strain_x + strain_z))
        szz = szz + DT * (stiff * strain_z + lame_lambda * (strain_x + strain_y))
        sxy = sxy + DT * shear_modulus * ((ahead_y(vx) - vx) + (ahead_x(vy) - vy))
        sxz = sxz + DT * shear_modulus * ((ahead_z(vx) - vx) + (ahead_x(vz) - vz))
        syz = syz + DT * shear_modulus * ((ahead_z(vy) - vy) + (ahead_y(vz) - vz))
        fault = jnp.where(fault_mask == 1, prestress + FRIC * rate - memory, sxy[:, center, :])
        sxy = sxy.at[:, center, :].set(fault)
        if step + 1 < STEPS:
            history = jnp.roll(jnp.concatenate([rate[None], history[:-1]], axis=0), CX, axis=2)
    return jnp.stack([vx, vy, vz]), jnp.stack([sxx, sxy, sxz, syz, szz, syy])
```

```python
import functools

import jax
import jax.numpy as jnp
from jax import lax
from jax.experimental import pallas as pl
from jax.experimental.pallas import tpu as pltpu
from jax.sharding import PartitionSpec as P

STEPS = 8
DT = 0.3
FRIC = 0.5
GROUP = 16

MESH = pl.DeviceIdType.MESH
F32 = jnp.float32


def kernel(
    n_strike,
    n_depth,
    vel_in,
    str_in,
    buoy,
    lam_ref,
    mu_ref,
    past,
    coefs,
    prestress,
    mask,
    vel,
    stress,
    pack0,
    pack1,
    accs,
    stage,
    got_r,
    got_l,
    got_rb,
    got_lt,
    got_t,
    got_b,
    got_acc,
    col_state,
    col_coef,
    layer_state,
    layer_coef,
    send_sem,
    recv_sem,
):
    nz, ny, nx = buoy.shape
    y0 = ny // 2
    hist = past.shape[0]
    s = lax.axis_index("strike")
    d = lax.axis_index("depth")
    left = lax.rem(s + n_strike - 1, n_strike)
    right = lax.rem(s + 1, n_strike)
    has_b = d > 0
    has_t = d < n_depth - 1
    below = jnp.maximum(d - 1, 0)
    above = jnp.minimum(d + 1, n_depth - 1)

    lane = lax.broadcasted_iota(jnp.int32, (ny, nx), 1)
    row = lax.broadcasted_iota(jnp.int32, (ny, nx), 0)
    first_lane, last_lane = lane == 0, lane == nx - 1
    first_row, last_row = row == 0, row == ny - 1

    def lanes_down(f, by):
        return pltpu.roll(f, (nx - by) % nx, 1)

    def ahead_x(f, column):
        return jnp.where(last_lane, column, pltpu.roll(f, nx - 1, 1))

    def behind_x(f, column):
        return jnp.where(first_lane, column, pltpu.roll(f, 1, 1))

    def ahead_y(f):
        return jnp.where(last_row, 0.0, pltpu.roll(f, ny - 1, 0))

    def behind_y(f):
        return jnp.where(first_row, 0.0, pltpu.roll(f, 1, 0))

    def col(f, group, z):
        at = group * GROUP + z
        return f[:, at : at + 1]

    def pack(columns):
        out = jnp.zeros((ny, nx), F32)
        for at, column in columns:
            out = jnp.where(lane == at, column, out)
        return out

    def copy(kind, slot, source=None):
        src, dst, to = (
            (pack0.at[slot], got_r.at[slot], (left, d)),
            (pack1.at[slot], got_l.at[slot], (right, d)),
            (pack0.at[slot], got_rb.at[slot], (left, above)),
            (pack1.at[slot], got_lt.at[slot], (right, below)),
            (vel.at[:, 0], got_t.at[slot], (s, below)),
            (vel.at[:, nz - 1], got_b.at[slot], (s, above)),
            (accs.at[slot], got_acc.at[slot], (right, d)),
        )[kind]
        return pltpu.make_async_remote_copy(
            src_ref=src if source is None else source,
            dst_ref=dst,
            send_sem=send_sem.at[kind, slot],
            recv_sem=recv_sem.at[kind, slot],
            device_id={"strike": to[0], "depth": to[1]},
            device_id_type=MESH,
        )

    sent_when = (None, None, has_t, has_b, has_b, has_t, None)
    got_when = (None, None, has_b, has_t, has_t, has_b, None)

    def guarded(condition, action):
        if condition is None:
            action()
        else:
            pl.when(condition)(action)

    def start(kind, slot, source=None):
        guarded(sent_when[kind], lambda: copy(kind, slot, source).start())

    def finish(kind, slot, source=None):
        guarded(got_when[kind], lambda: copy(kind, slot, source).wait_recv())
        guarded(sent_when[kind], lambda: copy(kind, slot, source).wait_send())

    barrier = pltpu.get_barrier_semaphore()

    def greet(strike, depth):
        pl.semaphore_signal(
            barrier,
            inc=1,
            device_id={"strike": strike, "depth": depth},
            device_id_type=MESH,
        )

    greet(left, d)
    greet(right, d)

    @pl.when(has_t)
    def _():
        greet(s, above)
        greet(left, above)

    @pl.when(has_b)
    def _():
        greet(s, below)
        greet(right, below)

    @pl.when(jnp.logical_not(has_t))
    def _():
        got_t[...] = jnp.zeros_like(got_t)
        got_lt[...] = jnp.zeros_like(got_lt)

    @pl.when(jnp.logical_not(has_b))
    def _():
        got_b[...] = jnp.zeros_like(got_b)
        got_rb[...] = jnp.zeros_like(got_rb)

    stage[0, 0] = str_in[4, 0]
    stage[0, 1] = lam_ref[0]
    stage[0, 2] = mu_ref[0]
    stage[1, 0] = str_in[2, nz - 1]
    stage[1, 1] = str_in[3, nz - 1]
    stage[1, 2] = mu_ref[nz - 1]
    heads, tails = [], []
    for z in range(nz):
        heads += [
            (z, str_in[0, z][:, :1]),
            (GROUP + z, lam_ref[z][:, :1]),
            (2 * GROUP + z, mu_ref[z][:, :1]),
        ]
        slides = mask[z : z + 1, :].astype(F32)
        tails += [
            (z, str_in[1, z][:, nx - 1 :]),
            (GROUP + z, str_in[2, z][:, nx - 1 :]),
            (2 * GROUP + z, mu_ref[z][:, nx - 1 :]),
            (3 * GROUP + z, slides[:, nx - 1 :]),
        ]
    pack0[1] = pack(heads)
    pack1[1] = pack(tails)
    pl.semaphore_wait(
        barrier, 2 + 2 * has_t.astype(jnp.int32) + 2 * has_b.astype(jnp.int32)
    )
    opening = ((4, stage.at[0]), (5, stage.at[1]), (0, None), (1, None))
    for kind, source in opening:
        start(kind, 1, source)

    vel[...] = vel_in[...]
    stress[...] = str_in[...]

    def add_past(m, sums):
        plane = past[m]
        return tuple(sums[t] + coefs[m + t] * plane for t in range(STEPS))

    sums = lax.fori_loop(
        0,
        hist - STEPS + 1,
        add_past,
        tuple(jnp.zeros((nz, nx), F32) for _ in range(STEPS)),
    )
    sums = list(sums)
    for m in range(hist - STEPS + 1, hist):
        for t in range(hist - m):
            sums[t] = sums[t] + coefs[m + t] * past[m]
    for t in range(STEPS):
        got_acc[1, t] = sums[t]

    for kind, source in opening:
        finish(kind, 1, source)
    r_init, l_init = got_r[1], got_l[1]
    col_state[0] = r_init
    col_state[1] = l_init
    col_state[2] = lanes_down(l_init, GROUP)
    col_coef[0] = lanes_down(r_init, GROUP)
    col_coef[1] = lanes_down(r_init, 2 * GROUP)
    col_coef[2] = lanes_down(l_init, 2 * GROUP)
    col_coef[3] = lanes_down(l_init, 3 * GROUP)
    layer_state[0] = got_t[1, 0]
    layer_state[1] = got_b[1, 0]
    layer_state[2] = got_b[1, 1]
    layer_coef[0] = got_t[1, 1]
    layer_coef[1] = got_t[1, 2]
    layer_coef[2] = got_b[1, 2]

    def step(j, carry):
        slot = lax.rem(j, 2)
        other = 1 - slot
        sxx_r, sxy_l, sxz_l = col_state[0], col_state[1], col_state[2]

        def velocity(z):
            sxx, sxy, sxz = stress[0, z], stress[1, z], stress[2, z]
            syz, szz, syy = stress[3, z], stress[4, z], stress[5, z]
            sxz_below = layer_state[1] if z == 0 else stress[2, z - 1]
            syz_below = layer_state[2] if z == 0 else stress[3, z - 1]
            szz_above = layer_state[0] if z == nz - 1 else stress[4, z + 1]
            scale = DT * buoy[z]
            vel[0, z] = vel[0, z] + scale * (
                ahead_x(sxx, col(sxx_r, 0, z)) - sxx + (sxy - behind_y(sxy)) + (sxz - sxz_below)
            )
            vel[1, z] = vel[1, z] + scale * (
                sxy - behind_x(sxy, col(sxy_l, 0, z)) + (ahead_y(syy) - syy) + (syz - syz_below)
            )
            vel[2, z] = vel[2, z] + scale * (
                sxz - behind_x(sxz, col(sxz_l, 0, z)) + (syz - behind_y(syz)) + (szz_above - szz)
            )

        velocity(0)
        start(4, slot)
        velocity(nz - 1)
        start(5, slot)
        for z in range(1, nz - 1):
            velocity(z)

        rate = jnp.concatenate(
            [vel[0, z, y0 + 1 : y0 + 2] - vel[0, z, y0 : y0 + 1] for z in range(nz)], axis=0
        )
        fault = prestress[...] + FRIC * rate - got_acc[other, 0]

        for t in range(STEPS - 1):
            accs[slot, t] = got_acc[other, t + 1] + coefs[t] * rate
        accs[slot, STEPS - 1] = jnp.zeros((nz, nx), F32)

        heads, tails = [], []
        for z in range(nz):
            for c in range(3):
                f = vel[c, z]
                heads.append((c * GROUP + z, f[:, :1]))
                tails.append((c * GROUP + z, f[:, nx - 1 :]))
            tails.append((3 * GROUP + z, fault[z : z + 1, nx - 1 :]))
        own_first = pack(heads)
        own_last = pack(tails)
        pack0[slot] = own_first
        pack1[slot] = own_last
        start(1, slot)
        start(0, slot)
        start(2, slot)
        start(3, slot)

        @pl.when(j < STEPS - 1)
        def _():
            copy(6, slot).start()

        for kind in range(6):
            finish(kind, slot)

        @pl.when(j < STEPS - 1)
        def _():
            finish(6, slot)

        got_first = jnp.where(
            lane == 2 * GROUP - 1, lanes_down(got_rb[slot], nz), got_r[slot]
        )
        got_last = jnp.where(lane == nz, pltpu.roll(got_lt[slot], nz, 1), got_l[slot])

        lam_r, mu_r, mu_l = col_coef[0], col_coef[1], col_coef[2]
        strain_x = got_first - own_last
        strain_y = lanes_down(got_first - behind_y(got_first), GROUP)
        strain_z = lanes_down(got_first - pltpu.roll(got_first, 1, 1), 2 * GROUP)
        col_state[0] = sxx_r + DT * (
            (lam_r + 2.0 * mu_r) * strain_x + lam_r * (strain_y + strain_z)
        )
        jump = own_first - got_last
        sheared = sxy_l + DT * mu_l * (ahead_y(got_last) - got_last + lanes_down(jump, GROUP))
        col_state[1] = jnp.where(
            jnp.logical_and(row == y0, col_coef[3] > 0.5),
            lanes_down(got_last, 3 * GROUP),
            sheared,
        )
        col_state[2] = sxz_l + DT * mu_l * (
            lanes_down(got_last, 1) - got_last + lanes_down(jump, 2 * GROUP)
        )

        top_x, top_y, top_z = got_t[slot, 0], got_t[slot, 1], got_t[slot, 2]
        lam_t, mu_t = layer_coef[0], layer_coef[1]
        layer_state[0] = layer_state[0] + DT * (
            (lam_t + 2.0 * mu_t) * (top_z - vel[2, nz - 1])
            + lam_t * (top_x - behind_x(top_x, col(got_last, 0, nz)) + (top_y - behind_y(top_y)))
        )
        low_x, low_y, low_z = got_b[slot, 0], got_b[slot, 1], got_b[slot, 2]
        low_mu = DT * layer_coef[2]
        layer_state[1] = layer_state[1] + low_mu * (
            vel[0, 0] - low_x + (ahead_x(low_z, col(got_first, 2, -1)) - low_z)
        )
        layer_state[2] = layer_state[2] + low_mu * (
            vel[1, 0] - low_y + (ahead_y(low_z) - low_z)
        )

        for z in range(nz):
            vx, vy, vz = vel[0, z], vel[1, z], vel[2, z]
            vz_below = low_z if z == 0 else vel[2, z - 1]
            vx_above = top_x if z == nz - 1 else vel[0, z + 1]
            vy_above = top_y if z == nz - 1 else vel[1, z + 1]
            lam, mu = DT * lam_ref[z], DT * mu_ref[z]
            twice = 2.0 * mu
            strain_x = vx - behind_x(vx, col(got_last, 0, z))
            strain_y = vy - behind_y(vy)
            strain_z = vz - vz_below
            spread = lam * (strain_x + strain_y + strain_z)
            stress[0, z] = stress[0, z] + (twice * strain_x + spread)
            stress[5, z] = stress[5, z] + (twice * strain_y + spread)
            stress[4, z] = stress[4, z] + (twice * strain_z + spread)
            sxy = stress[1, z] + mu * (
                ahead_y(vx) - vx + (ahead_x(vy, col(got_first, 1, z)) - vy)
            )
            stress[1, z] = sxy
            stress[1, z, y0 : y0 + 1] = jnp.where(
                mask[z : z + 1] == 1, fault[z : z + 1], sxy[y0 : y0 + 1]
            )
            stress[2, z] = stress[2, z] + mu * (
                vx_above - vx + (ahead_x(vz, col(got_first, 2, z)) - vz)
            )
            stress[3, z] = stress[3, z] + mu * (vy_above - vy + (ahead_y(vz) - vz))
        return carry

    lax.fori_loop(0, STEPS, step, 0)


def per_device(n_strike, n_depth, *args):
    nz, ny, nx = args[2].shape
    slab = (2, ny, nx)
    vmem = pl.BlockSpec(memory_space=pltpu.VMEM)
    specs = [vmem] * len(args)
    specs[6] = pl.BlockSpec(memory_space=pltpu.SMEM)
    return pl.pallas_call(
        functools.partial(kernel, n_strike, n_depth),
        out_shape=tuple(jax.ShapeDtypeStruct(a.shape, a.dtype) for a in args[:2]),
        in_specs=specs,
        out_specs=(vmem, vmem),
        scratch_shapes=[
            pltpu.VMEM(slab, F32),
            pltpu.VMEM(slab, F32),
            pltpu.VMEM((2, STEPS, nz, nx), F32),
            pltpu.VMEM((2, 3, ny, nx), F32),
            pltpu.VMEM(slab, F32),
            pltpu.VMEM(slab, F32),
            pltpu.VMEM(slab, F32),
            pltpu.VMEM(slab, F32),
            pltpu.VMEM((2, 3, ny, nx), F32),
            pltpu.VMEM((2, 3, ny, nx), F32),
            pltpu.VMEM((2, STEPS, nz, nx), F32),
            pltpu.VMEM((3, ny, nx), F32),
            pltpu.VMEM((4, ny, nx), F32),
            pltpu.VMEM((3, ny, nx), F32),
            pltpu.VMEM((3, ny, nx), F32),
            pltpu.SemaphoreType.DMA((7, 2)),
            pltpu.SemaphoreType.DMA((7, 2)),
        ],
        compiler_params=pltpu.CompilerParams(collective_id=0, has_side_effects=True),
    )(*args)


def solution(mesh):
    wide = P(None, "depth", None, "strike")
    placed = (
        wide,
        wide,
        P("depth", None, "strike"),
        P("depth", None, "strike"),
        P("depth", None, "strike"),
        P(None, "depth", "strike"),
        P(),
        P("depth", "strike"),
        P("depth", "strike"),
    )
    return jax.shard_map(
        functools.partial(per_device, mesh.shape["strike"], mesh.shape["depth"]),
        mesh=mesh,
        in_specs=placed,
        out_specs=(wide, wide),
        check_vma=False,
    )
```

```python
import functools

import jax
import jax.numpy as jnp
from jax import lax
from jax.experimental import pallas as pl
from jax.experimental.pallas import tpu as pltpu
from jax.sharding import PartitionSpec as P

STEPS = 8
DT = 0.3
FRIC = 0.5
GROUP = 16

MESH = pl.DeviceIdType.MESH
F32 = jnp.float32


def kernel(
    n_strike,
    n_depth,
    vel_in,
    str_in,
    buoy_in,
    lam_in,
    mu_in,
    past_in,
    coefs,
    prestress_in,
    mask_in,
    vel,
    stress,
    buoy,
    lam_ref,
    mu_ref,
    past,
    prestress,
    mask,
    pack0,
    pack1,
    accs,
    stage,
    got_r,
    got_l,
    got_rb,
    got_lt,
    got_t,
    got_b,
    got_acc,
    col_state,
    col_coef,
    layer_state,
    layer_coef,
    send_sem,
    recv_sem,
    load_sem,
):
    nz, ny, nx = buoy.shape
    y0 = ny // 2
    hist = past.shape[0]
    loads = [
        pltpu.make_async_copy(src, dst, load_sem.at[i])
        for i, (src, dst) in enumerate(
            (
                (str_in, stress),
                (lam_in, lam_ref),
                (mu_in, mu_ref),
                (mask_in, mask),
                (past_in, past),
                (vel_in, vel),
                (buoy_in, buoy),
                (prestress_in, prestress),
            )
        )
    ]
    for load in loads:
        load.start()

    s = lax.axis_index("strike")
    d = lax.axis_index("depth")
    left = lax.rem(s + n_strike - 1, n_strike)
    right = lax.rem(s + 1, n_strike)
    has_b = d > 0
    has_t = d < n_depth - 1
    below = jnp.maximum(d - 1, 0)
    above = jnp.minimum(d + 1, n_depth - 1)

    lane = lax.broadcasted_iota(jnp.int32, (ny, nx), 1)
    row = lax.broadcasted_iota(jnp.int32, (ny, nx), 0)
    first_lane, last_lane = lane == 0, lane == nx - 1
    first_row, last_row = row == 0, row == ny - 1

    def lanes_down(f, by):
        return pltpu.roll(f, (nx - by) % nx, 1)

    def ahead_x(f, column):
        return jnp.where(last_lane, column, pltpu.roll(f, nx - 1, 1))

    def behind_x(f, column):
        return jnp.where(first_lane, column, pltpu.roll(f, 1, 1))

    def ahead_y(f):
        return jnp.where(last_row, 0.0, pltpu.roll(f, ny - 1, 0))

    def behind_y(f):
        return jnp.where(first_row, 0.0, pltpu.roll(f, 1, 0))

    def col(f, group, z):
        at = group * GROUP + z
        return f[:, at : at + 1]

    def pack(columns):
        out = jnp.zeros((ny, nx), F32)
        for at, column in columns:
            out = jnp.where(lane == at, column, out)
        return out

    def copy(kind, slot, source=None):
        src, dst, to = (
            (pack0.at[slot], got_r.at[slot], (left, d)),
            (pack1.at[slot], got_l.at[slot], (right, d)),
            (pack0.at[slot], got_rb.at[slot], (left, above)),
            (pack1.at[slot], got_lt.at[slot], (right, below)),
            (vel.at[:, 0], got_t.at[slot], (s, below)),
            (vel.at[:, nz - 1], got_b.at[slot], (s, above)),
            (accs.at[slot], got_acc.at[slot], (right, d)),
        )[kind]
        return pltpu.make_async_remote_copy(
            src_ref=src if source is None else source,
            dst_ref=dst,
            send_sem=send_sem.at[kind, slot],
            recv_sem=recv_sem.at[kind, slot],
            device_id={"strike": to[0], "depth": to[1]},
            device_id_type=MESH,
        )

    sent_when = (None, None, has_t, has_b, has_b, has_t, None)
    got_when = (None, None, has_b, has_t, has_t, has_b, None)

    def guarded(condition, action):
        if condition is None:
            action()
        else:
            pl.when(condition)(action)

    def start(kind, slot, source=None):
        guarded(sent_when[kind], lambda: copy(kind, slot, source).start())

    def finish(kind, slot, source=None):
        guarded(got_when[kind], lambda: copy(kind, slot, source).wait_recv())
        guarded(sent_when[kind], lambda: copy(kind, slot, source).wait_send())

    barrier = pltpu.get_barrier_semaphore()

    def greet(strike, depth):
        pl.semaphore_signal(
            barrier,
            inc=1,
            device_id={"strike": strike, "depth": depth},
            device_id_type=MESH,
        )

    greet(left, d)
    greet(right, d)

    @pl.when(has_t)
    def _():
        greet(s, above)
        greet(left, above)

    @pl.when(has_b)
    def _():
        greet(s, below)
        greet(right, below)

    @pl.when(jnp.logical_not(has_t))
    def _():
        got_t[...] = jnp.zeros_like(got_t)
        got_lt[...] = jnp.zeros_like(got_lt)

    @pl.when(jnp.logical_not(has_b))
    def _():
        got_b[...] = jnp.zeros_like(got_b)
        got_rb[...] = jnp.zeros_like(got_rb)

    for load in loads[:4]:
        load.wait()
    stage[0, 0] = stress[4, 0]
    stage[0, 1] = lam_ref[0]
    stage[0, 2] = mu_ref[0]
    stage[1, 0] = stress[2, nz - 1]
    stage[1, 1] = stress[3, nz - 1]
    stage[1, 2] = mu_ref[nz - 1]
    heads, tails = [], []
    for z in range(nz):
        heads += [
            (z, stress[0, z][:, :1]),
            (GROUP + z, lam_ref[z][:, :1]),
            (2 * GROUP + z, mu_ref[z][:, :1]),
        ]
        slides = mask[z : z + 1, :].astype(F32)
        tails += [
            (z, stress[1, z][:, nx - 1 :]),
            (GROUP + z, stress[2, z][:, nx - 1 :]),
            (2 * GROUP + z, mu_ref[z][:, nx - 1 :]),
            (3 * GROUP + z, slides[:, nx - 1 :]),
        ]
    pack0[1] = pack(heads)
    pack1[1] = pack(tails)
    pl.semaphore_wait(
        barrier, 2 + 2 * has_t.astype(jnp.int32) + 2 * has_b.astype(jnp.int32)
    )
    opening = ((4, stage.at[0]), (5, stage.at[1]), (0, None), (1, None))
    for kind, source in opening:
        start(kind, 1, source)

    for load in loads[4:]:
        load.wait()

    def add_past(m, sums):
        plane = past[m]
        return tuple(sums[t] + coefs[m + t] * plane for t in range(STEPS))

    sums = lax.fori_loop(
        0,
        hist - STEPS + 1,
        add_past,
        tuple(jnp.zeros((nz, nx), F32) for _ in range(STEPS)),
    )
    sums = list(sums)
    for m in range(hist - STEPS + 1, hist):
        for t in range(hist - m):
            sums[t] = sums[t] + coefs[m + t] * past[m]
    for t in range(STEPS):
        got_acc[1, t] = sums[t]

    for kind, source in opening:
        finish(kind, 1, source)
    r_init, l_init = got_r[1], got_l[1]
    col_state[0] = r_init
    col_state[1] = l_init
    col_state[2] = lanes_down(l_init, GROUP)
    col_coef[0] = lanes_down(r_init, GROUP)
    col_coef[1] = lanes_down(r_init, 2 * GROUP)
    col_coef[2] = lanes_down(l_init, 2 * GROUP)
    col_coef[3] = lanes_down(l_init, 3 * GROUP)
    layer_state[0] = got_t[1, 0]
    layer_state[1] = got_b[1, 0]
    layer_state[2] = got_b[1, 1]
    layer_coef[0] = got_t[1, 1]
    layer_coef[1] = got_t[1, 2]
    layer_coef[2] = got_b[1, 2]

    def step(j, carry):
        slot = lax.rem(j, 2)
        other = 1 - slot
        sxx_r, sxy_l, sxz_l = col_state[0], col_state[1], col_state[2]

        def velocity(z):
            sxx, sxy, sxz = stress[0, z], stress[1, z], stress[2, z]
            syz, szz, syy = stress[3, z], stress[4, z], stress[5, z]
            sxz_below = layer_state[1] if z == 0 else stress[2, z - 1]
            syz_below = layer_state[2] if z == 0 else stress[3, z - 1]
            szz_above = layer_state[0] if z == nz - 1 else stress[4, z + 1]
            scale = DT * buoy[z]
            vel[0, z] = vel[0, z] + scale * (
                ahead_x(sxx, col(sxx_r, 0, z)) - sxx + (sxy - behind_y(sxy)) + (sxz - sxz_below)
            )
            vel[1, z] = vel[1, z] + scale * (
                sxy - behind_x(sxy, col(sxy_l, 0, z)) + (ahead_y(syy) - syy) + (syz - syz_below)
            )
            vel[2, z] = vel[2, z] + scale * (
                sxz - behind_x(sxz, col(sxz_l, 0, z)) + (syz - behind_y(syz)) + (szz_above - szz)
            )

        velocity(0)
        start(4, slot)
        velocity(nz - 1)
        start(5, slot)
        for z in range(1, nz - 1):
            velocity(z)

        rate = jnp.concatenate(
            [vel[0, z, y0 + 1 : y0 + 2] - vel[0, z, y0 : y0 + 1] for z in range(nz)], axis=0
        )
        fault = prestress[...] + FRIC * rate - got_acc[other, 0]

        for t in range(STEPS - 1):
            accs[slot, t] = got_acc[other, t + 1] + coefs[t] * rate
        accs[slot, STEPS - 1] = jnp.zeros((nz, nx), F32)

        heads, tails = [], []
        for z in range(nz):
            for c in range(3):
                f = vel[c, z]
                heads.append((c * GROUP + z, f[:, :1]))
                tails.append((c * GROUP + z, f[:, nx - 1 :]))
            tails.append((3 * GROUP + z, fault[z : z + 1, nx - 1 :]))
        own_first = pack(heads)
        own_last = pack(tails)
        pack0[slot] = own_first
        pack1[slot] = own_last
        start(1, slot)
        start(0, slot)
        start(2, slot)
        start(3, slot)

        @pl.when(j < STEPS - 1)
        def _():
            copy(6, slot).start()

        def strain(z, low_z, top_x, top_y):
            vx, vy, vz = vel[0, z], vel[1, z], vel[2, z]
            vz_below = low_z if z == 0 else vel[2, z - 1]
            vx_above = top_x if z == nz - 1 else vel[0, z + 1]
            vy_above = top_y if z == nz - 1 else vel[1, z + 1]
            lam, mu = DT * lam_ref[z], DT * mu_ref[z]
            twice = 2.0 * mu
            strain_x = vx - behind_x(vx, 0.0)
            strain_y = vy - behind_y(vy)
            strain_z = vz - vz_below
            spread = lam * (strain_x + strain_y + strain_z)
            stress[0, z] = stress[0, z] + (twice * strain_x + spread)
            stress[5, z] = stress[5, z] + (twice * strain_y + spread)
            stress[4, z] = stress[4, z] + (twice * strain_z + spread)
            stress[1, z] = stress[1, z] + mu * (ahead_y(vx) - vx + (ahead_x(vy, 0.0) - vy))
            stress[2, z] = stress[2, z] + mu * (vx_above - vx + (ahead_x(vz, 0.0) - vz))
            stress[3, z] = stress[3, z] + mu * (vy_above - vy + (ahead_y(vz) - vz))

        for z in range(1, nz - 1):
            strain(z, None, None, None)
        finish(4, slot)
        finish(5, slot)
        top_x, top_y, top_z = got_t[slot, 0], got_t[slot, 1], got_t[slot, 2]
        low_x, low_y, low_z = got_b[slot, 0], got_b[slot, 1], got_b[slot, 2]
        strain(0, low_z, top_x, top_y)
        strain(nz - 1, low_z, top_x, top_y)

        finish(0, slot)
        finish(1, slot)
        column_r, column_l = got_r[slot], got_l[slot]
        for z in range(nz):
            lam, mu = DT * lam_ref[z], DT * mu_ref[z]
            behind = jnp.where(first_lane, -col(column_l, 0, z), 0.0)
            spread = lam * behind
            stress[0, z] = stress[0, z] + (2.0 * mu * behind + spread)
            stress[5, z] = stress[5, z] + spread
            stress[4, z] = stress[4, z] + spread
            sxy = stress[1, z] + mu * jnp.where(last_lane, col(column_r, 1, z), 0.0)
            stress[1, z] = sxy
            stress[1, z, y0 : y0 + 1] = jnp.where(
                mask[z : z + 1] == 1, fault[z : z + 1], sxy[y0 : y0 + 1]
            )
            stress[2, z] = stress[2, z] + mu * jnp.where(
                last_lane, col(column_r, 2, z), 0.0
            )

        finish(2, slot)
        finish(3, slot)

        @pl.when(j < STEPS - 1)
        def _():
            finish(6, slot)

        got_first = jnp.where(
            lane == 2 * GROUP - 1, lanes_down(got_rb[slot], nz), column_r
        )
        got_last = jnp.where(lane == nz, pltpu.roll(got_lt[slot], nz, 1), column_l)

        lam_r, mu_r, mu_l = col_coef[0], col_coef[1], col_coef[2]
        strain_x = got_first - own_last
        strain_y = lanes_down(got_first - behind_y(got_first), GROUP)
        strain_z = lanes_down(got_first - pltpu.roll(got_first, 1, 1), 2 * GROUP)
        col_state[0] = sxx_r + DT * (
            (lam_r + 2.0 * mu_r) * strain_x + lam_r * (strain_y + strain_z)
        )
        jump = own_first - got_last
        sheared = sxy_l + DT * mu_l * (ahead_y(got_last) - got_last + lanes_down(jump, GROUP))
        col_state[1] = jnp.where(
            jnp.logical_and(row == y0, col_coef[3] > 0.5),
            lanes_down(got_last, 3 * GROUP),
            sheared,
        )
        col_state[2] = sxz_l + DT * mu_l * (
            lanes_down(got_last, 1) - got_last + lanes_down(jump, 2 * GROUP)
        )

        lam_t, mu_t = layer_coef[0], layer_coef[1]
        layer_state[0] = layer_state[0] + DT * (
            (lam_t + 2.0 * mu_t) * (top_z - vel[2, nz - 1])
            + lam_t * (top_x - behind_x(top_x, col(got_last, 0, nz)) + (top_y - behind_y(top_y)))
        )
        low_mu = DT * layer_coef[2]
        layer_state[1] = layer_state[1] + low_mu * (
            vel[0, 0] - low_x + (ahead_x(low_z, col(got_first, 2, -1)) - low_z)
        )
        layer_state[2] = layer_state[2] + low_mu * (
            vel[1, 0] - low_y + (ahead_y(low_z) - low_z)
        )
        return carry

    lax.fori_loop(0, STEPS, step, 0)


def per_device(n_strike, n_depth, *args):
    nz, ny, nx = args[2].shape
    slab = (2, ny, nx)
    vmem = pl.BlockSpec(memory_space=pltpu.VMEM)
    specs = [pl.BlockSpec(memory_space=pl.ANY)] * len(args)
    specs[6] = pl.BlockSpec(memory_space=pltpu.SMEM)
    return pl.pallas_call(
        functools.partial(kernel, n_strike, n_depth),
        out_shape=tuple(jax.ShapeDtypeStruct(a.shape, a.dtype) for a in args[:2]),
        in_specs=specs,
        out_specs=(vmem, vmem),
        scratch_shapes=[
            *(pltpu.VMEM(args[i].shape, args[i].dtype) for i in (2, 3, 4, 5, 7, 8)),
            pltpu.VMEM(slab, F32),
            pltpu.VMEM(slab, F32),
            pltpu.VMEM((2, STEPS, nz, nx), F32),
            pltpu.VMEM((2, 3, ny, nx), F32),
            pltpu.VMEM(slab, F32),
            pltpu.VMEM(slab, F32),
            pltpu.VMEM(slab, F32),
            pltpu.VMEM(slab, F32),
            pltpu.VMEM((2, 3, ny, nx), F32),
            pltpu.VMEM((2, 3, ny, nx), F32),
            pltpu.VMEM((2, STEPS, nz, nx), F32),
            pltpu.VMEM((3, ny, nx), F32),
            pltpu.VMEM((4, ny, nx), F32),
            pltpu.VMEM((3, ny, nx), F32),
            pltpu.VMEM((3, ny, nx), F32),
            pltpu.SemaphoreType.DMA((7, 2)),
            pltpu.SemaphoreType.DMA((7, 2)),
            pltpu.SemaphoreType.DMA((8,)),
        ],
        compiler_params=pltpu.CompilerParams(collective_id=0, has_side_effects=True),
    )(*args)


def solution(mesh):
    wide = P(None, "depth", None, "strike")
    placed = (
        wide,
        wide,
        P("depth", None, "strike"),
        P("depth", None, "strike"),
        P("depth", None, "strike"),
        P(None, "depth", "strike"),
        P(),
        P("depth", "strike"),
        P("depth", "strike"),
    )
    return jax.shard_map(
        functools.partial(per_device, mesh.shape["strike"], mesh.shape["depth"]),
        mesh=mesh,
        in_specs=placed,
        out_specs=(wide, wide),
        check_vma=False,
    )
```

```python
import functools

import jax
import jax.numpy as jnp
from jax import lax
from jax.experimental import pallas as pl
from jax.experimental.pallas import tpu as pltpu
from jax.sharding import PartitionSpec as P

STEPS = 8
DT = 0.3
FRIC = 0.5
GROUP = 16

MESH = pl.DeviceIdType.MESH
F32 = jnp.float32


def kernel(
    n_strike,
    n_depth,
    vel_in,
    str_in,
    buoy_in,
    lam_in,
    mu_in,
    past_in,
    coefs,
    prestress_in,
    mask_in,
    vel,
    stress,
    buoy,
    lam_ref,
    mu_ref,
    past,
    prestress,
    mask,
    pack0,
    pack1,
    accs,
    stage,
    got_r,
    got_l,
    got_rb,
    got_lt,
    got_t,
    got_b,
    got_acc,
    col_state,
    col_coef,
    layer_state,
    layer_coef,
    send_sem,
    recv_sem,
    load_sem,
):
    nz, ny, nx = buoy.shape
    y0 = ny // 2
    hist = past.shape[0]
    loads = [
        pltpu.make_async_copy(src, dst, load_sem.at[i])
        for i, (src, dst) in enumerate(
            (
                (str_in, stress),
                (lam_in, lam_ref),
                (mu_in, mu_ref),
                (mask_in, mask),
                (past_in, past),
                (vel_in, vel),
                (buoy_in, buoy),
                (prestress_in, prestress),
            )
        )
    ]
    for load in loads:
        load.start()

    s = lax.axis_index("strike")
    d = lax.axis_index("depth")
    left = lax.rem(s + n_strike - 1, n_strike)
    right = lax.rem(s + 1, n_strike)
    has_b = d > 0
    has_t = d < n_depth - 1
    below = jnp.maximum(d - 1, 0)
    above = jnp.minimum(d + 1, n_depth - 1)

    lane = lax.broadcasted_iota(jnp.int32, (ny, nx), 1)
    row = lax.broadcasted_iota(jnp.int32, (ny, nx), 0)
    first_lane, last_lane = lane == 0, lane == nx - 1
    first_row, last_row = row == 0, row == ny - 1

    def lanes_down(f, by):
        return pltpu.roll(f, (nx - by) % nx, 1)

    def ahead_x(f, column):
        return jnp.where(last_lane, column, pltpu.roll(f, nx - 1, 1))

    def behind_x(f, column):
        return jnp.where(first_lane, column, pltpu.roll(f, 1, 1))

    def ahead_y(f):
        return jnp.where(last_row, 0.0, pltpu.roll(f, ny - 1, 0))

    def behind_y(f):
        return jnp.where(first_row, 0.0, pltpu.roll(f, 1, 0))

    def col(f, group, z):
        at = group * GROUP + z
        return f[:, at : at + 1]

    def pack(columns):
        out = jnp.zeros((ny, nx), F32)
        for at, column in columns:
            out = jnp.where(lane == at, column, out)
        return out

    def copy(kind, slot, source=None):
        src, dst, to = (
            (pack0.at[slot], got_r.at[slot], (left, d)),
            (pack1.at[slot], got_l.at[slot], (right, d)),
            (pack0.at[slot], got_rb.at[slot], (left, above)),
            (pack1.at[slot], got_lt.at[slot], (right, below)),
            (vel.at[:, 0], got_t.at[slot], (s, below)),
            (vel.at[:, nz - 1], got_b.at[slot], (s, above)),
            (accs.at[slot], got_acc.at[slot], (right, d)),
        )[kind]
        return pltpu.make_async_remote_copy(
            src_ref=src if source is None else source,
            dst_ref=dst,
            send_sem=send_sem.at[kind, slot],
            recv_sem=recv_sem.at[kind, slot],
            device_id={"strike": to[0], "depth": to[1]},
            device_id_type=MESH,
        )

    sent_when = (None, None, has_t, has_b, has_b, has_t, None)
    got_when = (None, None, has_b, has_t, has_t, has_b, None)

    def guarded(condition, action):
        if condition is None:
            action()
        else:
            pl.when(condition)(action)

    def start(kind, slot, source=None):
        guarded(sent_when[kind], lambda: copy(kind, slot, source).start())

    def finish(kind, slot, source=None):
        guarded(got_when[kind], lambda: copy(kind, slot, source).wait_recv())
        guarded(sent_when[kind], lambda: copy(kind, slot, source).wait_send())

    barrier = pltpu.get_barrier_semaphore()

    def greet(strike, depth):
        pl.semaphore_signal(
            barrier,
            inc=1,
            device_id={"strike": strike, "depth": depth},
            device_id_type=MESH,
        )

    greet(left, d)
    greet(right, d)

    @pl.when(has_t)
    def _():
        greet(s, above)
        greet(left, above)

    @pl.when(has_b)
    def _():
        greet(s, below)
        greet(right, below)

    @pl.when(jnp.logical_not(has_t))
    def _():
        got_t[...] = jnp.zeros_like(got_t)
        got_lt[...] = jnp.zeros_like(got_lt)

    @pl.when(jnp.logical_not(has_b))
    def _():
        got_b[...] = jnp.zeros_like(got_b)
        got_rb[...] = jnp.zeros_like(got_rb)

    for load in loads[:4]:
        load.wait()
    stage[0, 0] = stress[4, 0]
    stage[0, 1] = lam_ref[0]
    stage[0, 2] = mu_ref[0]
    stage[1, 0] = stress[2, nz - 1]
    stage[1, 1] = stress[3, nz - 1]
    stage[1, 2] = mu_ref[nz - 1]
    heads, tails = [], []
    for z in range(nz):
        heads += [
            (z, stress[0, z][:, :1]),
            (GROUP + z, lam_ref[z][:, :1]),
            (2 * GROUP + z, mu_ref[z][:, :1]),
        ]
        slides = mask[z : z + 1, :].astype(F32)
        tails += [
            (z, stress[1, z][:, nx - 1 :]),
            (GROUP + z, stress[2, z][:, nx - 1 :]),
            (2 * GROUP + z, mu_ref[z][:, nx - 1 :]),
            (3 * GROUP + z, slides[:, nx - 1 :]),
        ]
    pack0[1] = pack(heads)
    pack1[1] = pack(tails)
    pl.semaphore_wait(
        barrier, 2 + 2 * has_t.astype(jnp.int32) + 2 * has_b.astype(jnp.int32)
    )
    opening = ((4, stage.at[0]), (5, stage.at[1]), (0, None), (1, None))
    for kind, source in opening:
        start(kind, 1, source)

    for load in loads[4:]:
        load.wait()

    def add_past(m, sums):
        plane = past[m]
        return tuple(sums[t] + coefs[m + t] * plane for t in range(STEPS))

    sums = lax.fori_loop(
        0,
        hist - STEPS + 1,
        add_past,
        tuple(jnp.zeros((nz, nx), F32) for _ in range(STEPS)),
    )
    sums = list(sums)
    for m in range(hist - STEPS + 1, hist):
        for t in range(hist - m):
            sums[t] = sums[t] + coefs[m + t] * past[m]
    for t in range(STEPS):
        got_acc[1, t] = sums[t]

    for kind, source in opening:
        finish(kind, 1, source)
    r_init, l_init = got_r[1], got_l[1]
    col_state[0] = r_init
    col_state[1] = l_init
    col_state[2] = lanes_down(l_init, GROUP)
    col_coef[0] = lanes_down(r_init, GROUP)
    col_coef[1] = lanes_down(r_init, 2 * GROUP)
    col_coef[2] = lanes_down(l_init, 2 * GROUP)
    col_coef[3] = lanes_down(l_init, 3 * GROUP)
    layer_state[0] = got_t[1, 0]
    layer_state[1] = got_b[1, 0]
    layer_state[2] = got_b[1, 1]
    layer_coef[0] = got_t[1, 1]
    layer_coef[1] = got_t[1, 2]
    layer_coef[2] = got_b[1, 2]

    def step(j, carry):
        slot = lax.rem(j, 2)
        other = 1 - slot
        def velocity(z):
            sxx_r, sxy_l, sxz_l = col_state[0], col_state[1], col_state[2]
            sxx, sxy, sxz = stress[0, z], stress[1, z], stress[2, z]
            syz, szz, syy = stress[3, z], stress[4, z], stress[5, z]
            sxz_below = layer_state[1] if z == 0 else stress[2, z - 1]
            syz_below = layer_state[2] if z == 0 else stress[3, z - 1]
            szz_above = layer_state[0] if z == nz - 1 else stress[4, z + 1]
            scale = DT * buoy[z]
            vel[0, z] = vel[0, z] + scale * (
                ahead_x(sxx, col(sxx_r, 0, z)) - sxx + (sxy - behind_y(sxy)) + (sxz - sxz_below)
            )
            vel[1, z] = vel[1, z] + scale * (
                sxy - behind_x(sxy, col(sxy_l, 0, z)) + (ahead_y(syy) - syy) + (syz - syz_below)
            )
            vel[2, z] = vel[2, z] + scale * (
                sxz - behind_x(sxz, col(sxz_l, 0, z)) + (syz - behind_y(syz)) + (szz_above - szz)
            )

        for z in range(1, nz - 1):
            velocity(z)

        @pl.when(j > 0)
        def _():
            for kind in (2, 3, 6):
                finish(kind, other)
            vz_corner, vx_corner = got_rb[other], got_lt[other]
            at = 2 * GROUP + nz - 1
            col_state[0] = col_state[0] - DT * col_coef[0] * jnp.where(
                first_lane, vz_corner[:, at : at + 1], 0.0
            )
            col_state[2] = col_state[2] + DT * col_coef[2] * jnp.where(
                lane == nz - 1, vx_corner[:, :1], 0.0
            )
            layer_state[0] = layer_state[0] - DT * layer_coef[0] * jnp.where(
                first_lane, vx_corner[:, :1], 0.0
            )
            layer_state[1] = layer_state[1] + DT * layer_coef[2] * jnp.where(
                last_lane, vz_corner[:, at : at + 1], 0.0
            )

        velocity(0)
        start(4, slot)
        velocity(nz - 1)
        start(5, slot)

        rate = jnp.concatenate(
            [vel[0, z, y0 + 1 : y0 + 2] - vel[0, z, y0 : y0 + 1] for z in range(nz)], axis=0
        )
        fault = prestress[...] + FRIC * rate - got_acc[other, 0]

        for t in range(STEPS - 1):
            accs[slot, t] = got_acc[other, t + 1] + coefs[t] * rate
        accs[slot, STEPS - 1] = jnp.zeros((nz, nx), F32)

        heads, tails = [], []
        for z in range(nz):
            for c in range(3):
                f = vel[c, z]
                heads.append((c * GROUP + z, f[:, :1]))
                tails.append((c * GROUP + z, f[:, nx - 1 :]))
            tails.append((3 * GROUP + z, fault[z : z + 1, nx - 1 :]))
        own_first = pack(heads)
        own_last = pack(tails)
        pack0[slot] = own_first
        pack1[slot] = own_last
        start(1, slot)
        start(0, slot)

        @pl.when(j < STEPS - 1)
        def _():
            for kind in (2, 3, 6):
                start(kind, slot)

        def strain(z, low_z, top_x, top_y):
            vx, vy, vz = vel[0, z], vel[1, z], vel[2, z]
            vz_below = low_z if z == 0 else vel[2, z - 1]
            vx_above = top_x if z == nz - 1 else vel[0, z + 1]
            vy_above = top_y if z == nz - 1 else vel[1, z + 1]
            lam, mu = DT * lam_ref[z], DT * mu_ref[z]
            twice = 2.0 * mu
            strain_x = vx - behind_x(vx, 0.0)
            strain_y = vy - behind_y(vy)
            strain_z = vz - vz_below
            spread = lam * (strain_x + strain_y + strain_z)
            stress[0, z] = stress[0, z] + (twice * strain_x + spread)
            stress[5, z] = stress[5, z] + (twice * strain_y + spread)
            stress[4, z] = stress[4, z] + (twice * strain_z + spread)
            stress[1, z] = stress[1, z] + mu * (ahead_y(vx) - vx + (ahead_x(vy, 0.0) - vy))
            stress[2, z] = stress[2, z] + mu * (vx_above - vx + (ahead_x(vz, 0.0) - vz))
            stress[3, z] = stress[3, z] + mu * (vy_above - vy + (ahead_y(vz) - vz))

        for z in range(1, nz - 1):
            strain(z, None, None, None)
        finish(4, slot)
        finish(5, slot)
        top_x, top_y, top_z = got_t[slot, 0], got_t[slot, 1], got_t[slot, 2]
        low_x, low_y, low_z = got_b[slot, 0], got_b[slot, 1], got_b[slot, 2]
        strain(0, low_z, top_x, top_y)
        strain(nz - 1, low_z, top_x, top_y)

        finish(0, slot)
        finish(1, slot)
        column_r, column_l = got_r[slot], got_l[slot]
        for z in range(nz):
            lam, mu = DT * lam_ref[z], DT * mu_ref[z]
            behind = jnp.where(first_lane, -col(column_l, 0, z), 0.0)
            spread = lam * behind
            stress[0, z] = stress[0, z] + (2.0 * mu * behind + spread)
            stress[5, z] = stress[5, z] + spread
            stress[4, z] = stress[4, z] + spread
            sxy = stress[1, z] + mu * jnp.where(last_lane, col(column_r, 1, z), 0.0)
            stress[1, z] = sxy
            stress[1, z, y0 : y0 + 1] = jnp.where(
                mask[z : z + 1] == 1, fault[z : z + 1], sxy[y0 : y0 + 1]
            )
            stress[2, z] = stress[2, z] + mu * jnp.where(
                last_lane, col(column_r, 2, z), 0.0
            )

        got_first, got_last = column_r, column_l

        lam_r, mu_r, mu_l = col_coef[0], col_coef[1], col_coef[2]
        strain_x = got_first - own_last
        strain_y = lanes_down(got_first - behind_y(got_first), GROUP)
        strain_z = lanes_down(got_first - pltpu.roll(got_first, 1, 1), 2 * GROUP)
        col_state[0] = col_state[0] + DT * (
            (lam_r + 2.0 * mu_r) * strain_x + lam_r * (strain_y + strain_z)
        )
        jump = own_first - got_last
        sheared = col_state[1] + DT * mu_l * (ahead_y(got_last) - got_last + lanes_down(jump, GROUP))
        col_state[1] = jnp.where(
            jnp.logical_and(row == y0, col_coef[3] > 0.5),
            lanes_down(got_last, 3 * GROUP),
            sheared,
        )
        col_state[2] = col_state[2] + DT * mu_l * (
            lanes_down(got_last, 1) - got_last + lanes_down(jump, 2 * GROUP)
        )

        lam_t, mu_t = layer_coef[0], layer_coef[1]
        layer_state[0] = layer_state[0] + DT * (
            (lam_t + 2.0 * mu_t) * (top_z - vel[2, nz - 1])
            + lam_t * (top_x - behind_x(top_x, 0.0) + (top_y - behind_y(top_y)))
        )
        low_mu = DT * layer_coef[2]
        layer_state[1] = layer_state[1] + low_mu * (
            vel[0, 0] - low_x + (ahead_x(low_z, 0.0) - low_z)
        )
        layer_state[2] = layer_state[2] + low_mu * (
            vel[1, 0] - low_y + (ahead_y(low_z) - low_z)
        )
        return carry

    lax.fori_loop(0, STEPS, step, 0)


def per_device(n_strike, n_depth, *args):
    nz, ny, nx = args[2].shape
    slab = (2, ny, nx)
    vmem = pl.BlockSpec(memory_space=pltpu.VMEM)
    specs = [pl.BlockSpec(memory_space=pl.ANY)] * len(args)
    specs[6] = pl.BlockSpec(memory_space=pltpu.SMEM)
    return pl.pallas_call(
        functools.partial(kernel, n_strike, n_depth),
        out_shape=tuple(jax.ShapeDtypeStruct(a.shape, a.dtype) for a in args[:2]),
        in_specs=specs,
        out_specs=(vmem, vmem),
        scratch_shapes=[
            *(pltpu.VMEM(args[i].shape, args[i].dtype) for i in (2, 3, 4, 5, 7, 8)),
            pltpu.VMEM(slab, F32),
            pltpu.VMEM(slab, F32),
            pltpu.VMEM((2, STEPS, nz, nx), F32),
            pltpu.VMEM((2, 3, ny, nx), F32),
            pltpu.VMEM(slab, F32),
            pltpu.VMEM(slab, F32),
            pltpu.VMEM(slab, F32),
            pltpu.VMEM(slab, F32),
            pltpu.VMEM((2, 3, ny, nx), F32),
            pltpu.VMEM((2, 3, ny, nx), F32),
            pltpu.VMEM((2, STEPS, nz, nx), F32),
            pltpu.VMEM((3, ny, nx), F32),
            pltpu.VMEM((4, ny, nx), F32),
            pltpu.VMEM((3, ny, nx), F32),
            pltpu.VMEM((3, ny, nx), F32),
            pltpu.SemaphoreType.DMA((7, 2)),
            pltpu.SemaphoreType.DMA((7, 2)),
            pltpu.SemaphoreType.DMA((8,)),
        ],
        compiler_params=pltpu.CompilerParams(collective_id=0, has_side_effects=True),
    )(*args)


def solution(mesh):
    wide = P(None, "depth", None, "strike")
    placed = (
        wide,
        wide,
        P("depth", None, "strike"),
        P("depth", None, "strike"),
        P("depth", None, "strike"),
        P(None, "depth", "strike"),
        P(),
        P("depth", "strike"),
        P("depth", "strike"),
    )
    return jax.shard_map(
        functools.partial(per_device, mesh.shape["strike"], mesh.shape["depth"]),
        mesh=mesh,
        in_specs=placed,
        out_specs=(wide, wide),
        check_vma=False,
    )
```

```python
import functools

import jax
import jax.numpy as jnp
from jax import lax
from jax.experimental import pallas as pl
from jax.experimental.pallas import tpu as pltpu
from jax.sharding import PartitionSpec as P

STEPS = 8
DT = 0.3
FRIC = 0.5
GROUP = 16

MESH = pl.DeviceIdType.MESH
F32 = jnp.float32


def kernel(
    n_strike,
    n_depth,
    vel_in,
    str_in,
    buoy_in,
    lam_in,
    mu_in,
    past_in,
    coefs,
    prestress_in,
    mask_in,
    vel,
    stress,
    buoy,
    lam_ref,
    mu_ref,
    past,
    prestress,
    mask,
    pack0,
    pack1,
    accs,
    stage,
    got_r,
    got_l,
    got_rb,
    got_lt,
    got_t,
    got_b,
    got_acc,
    col_state,
    col_coef,
    layer_state,
    layer_coef,
    send_sem,
    recv_sem,
    load_sem,
):
    nz, ny, nx = buoy.shape
    y0 = ny // 2
    hist = past.shape[0]
    loads = [
        pltpu.make_async_copy(src, dst, load_sem.at[i])
        for i, (src, dst) in enumerate(
            (
                (str_in, stress),
                (lam_in, lam_ref),
                (mu_in, mu_ref),
                (mask_in, mask),
                (past_in, past),
                (vel_in, vel),
                (buoy_in, buoy),
                (prestress_in, prestress),
            )
        )
    ]
    for load in loads:
        load.start()

    s = lax.axis_index("strike")
    d = lax.axis_index("depth")
    left = lax.rem(s + n_strike - 1, n_strike)
    right = lax.rem(s + 1, n_strike)
    has_b = d > 0
    has_t = d < n_depth - 1
    below = jnp.maximum(d - 1, 0)
    above = jnp.minimum(d + 1, n_depth - 1)

    lane = lax.broadcasted_iota(jnp.int32, (ny, nx), 1)
    row = lax.broadcasted_iota(jnp.int32, (ny, nx), 0)
    first_lane, last_lane = lane == 0, lane == nx - 1
    first_row, last_row = row == 0, row == ny - 1

    def lanes_down(f, by):
        return pltpu.roll(f, (nx - by) % nx, 1)

    def ahead_x(f, column):
        return jnp.where(last_lane, column, pltpu.roll(f, nx - 1, 1))

    def behind_x(f, column):
        return jnp.where(first_lane, column, pltpu.roll(f, 1, 1))

    def ahead_y(f):
        return jnp.where(last_row, 0.0, pltpu.roll(f, ny - 1, 0))

    def behind_y(f):
        return jnp.where(first_row, 0.0, pltpu.roll(f, 1, 0))

    def col(f, group, z):
        at = group * GROUP + z
        return f[:, at : at + 1]

    def pack(columns):
        out = jnp.zeros((ny, nx), F32)
        for at, column in columns:
            out = jnp.where(lane == at, column, out)
        return out

    def copy(kind, slot, source=None):
        src, dst, to = (
            (pack0.at[slot], got_r.at[slot], (left, d)),
            (pack1.at[slot], got_l.at[slot], (right, d)),
            (pack0.at[slot], got_rb.at[slot], (left, above)),
            (pack1.at[slot], got_lt.at[slot], (right, below)),
            (vel.at[:, 0], got_t.at[slot], (s, below)),
            (vel.at[:, nz - 1], got_b.at[slot], (s, above)),
            (accs.at[slot], got_acc.at[slot], (right, d)),
        )[kind]
        return pltpu.make_async_remote_copy(
            src_ref=src if source is None else source,
            dst_ref=dst,
            send_sem=send_sem.at[kind, slot],
            recv_sem=recv_sem.at[kind, slot],
            device_id={"strike": to[0], "depth": to[1]},
            device_id_type=MESH,
        )

    sent_when = (None, None, has_t, has_b, has_b, has_t, None)
    got_when = (None, None, has_b, has_t, has_t, has_b, None)

    def guarded(condition, action):
        if condition is None:
            action()
        else:
            pl.when(condition)(action)

    def start(kind, slot, source=None):
        guarded(sent_when[kind], lambda: copy(kind, slot, source).start())

    def finish(kind, slot, source=None):
        guarded(got_when[kind], lambda: copy(kind, slot, source).wait_recv())
        guarded(sent_when[kind], lambda: copy(kind, slot, source).wait_send())

    barrier = pltpu.get_barrier_semaphore()

    def greet(strike, depth):
        pl.semaphore_signal(
            barrier,
            inc=1,
            device_id={"strike": strike, "depth": depth},
            device_id_type=MESH,
        )

    greet(left, d)
    greet(right, d)

    @pl.when(has_t)
    def _():
        greet(s, above)
        greet(left, above)

    @pl.when(has_b)
    def _():
        greet(s, below)
        greet(right, below)

    @pl.when(jnp.logical_not(has_t))
    def _():
        got_t[...] = jnp.zeros_like(got_t)
        got_lt[...] = jnp.zeros_like(got_lt)

    @pl.when(jnp.logical_not(has_b))
    def _():
        got_b[...] = jnp.zeros_like(got_b)
        got_rb[...] = jnp.zeros_like(got_rb)

    for load in loads[:4]:
        load.wait()
    stage[0, 0] = stress[4, 0]
    stage[0, 1] = lam_ref[0]
    stage[0, 2] = mu_ref[0]
    stage[1, 0] = stress[2, nz - 1]
    stage[1, 1] = stress[3, nz - 1]
    stage[1, 2] = mu_ref[nz - 1]
    heads, tails = [], []
    for z in range(nz):
        heads += [
            (z, stress[0, z][:, :1]),
            (GROUP + z, lam_ref[z][:, :1]),
            (2 * GROUP + z, mu_ref[z][:, :1]),
        ]
        slides = mask[z : z + 1, :].astype(F32)
        tails += [
            (z, stress[1, z][:, nx - 1 :]),
            (GROUP + z, stress[2, z][:, nx - 1 :]),
            (2 * GROUP + z, mu_ref[z][:, nx - 1 :]),
            (3 * GROUP + z, slides[:, nx - 1 :]),
        ]
    pack0[1] = pack(heads)
    pack1[1] = pack(tails)
    pl.semaphore_wait(
        barrier, 2 + 2 * has_t.astype(jnp.int32) + 2 * has_b.astype(jnp.int32)
    )
    opening = ((4, stage.at[0]), (5, stage.at[1]), (0, None), (1, None))
    for kind, source in opening:
        start(kind, 1, source)

    for load in loads[4:]:
        load.wait()

    def add_past(m, sums):
        plane = past[m]
        return tuple(sums[t] + coefs[m + t] * plane for t in range(STEPS))

    sums = lax.fori_loop(
        0,
        hist - STEPS + 1,
        add_past,
        tuple(jnp.zeros((nz, nx), F32) for _ in range(STEPS)),
    )
    sums = list(sums)
    for m in range(hist - STEPS + 1, hist):
        for t in range(hist - m):
            sums[t] = sums[t] + coefs[m + t] * past[m]
    for t in range(STEPS):
        got_acc[1, t] = sums[t]

    for kind, source in opening:
        finish(kind, 1, source)
    r_init, l_init = got_r[1], got_l[1]
    col_state[0] = r_init
    col_state[1] = l_init
    col_state[2] = lanes_down(l_init, GROUP)
    col_coef[0] = lanes_down(r_init, GROUP)
    col_coef[1] = lanes_down(r_init, 2 * GROUP)
    col_coef[2] = lanes_down(l_init, 2 * GROUP)
    col_coef[3] = lanes_down(l_init, 3 * GROUP)
    layer_state[0] = got_t[1, 0]
    layer_state[1] = got_b[1, 0]
    layer_state[2] = got_b[1, 1]
    layer_coef[0] = got_t[1, 1]
    layer_coef[1] = got_t[1, 2]
    layer_coef[2] = got_b[1, 2]

    def step(j, carry):
        slot = lax.rem(j, 2)
        other = 1 - slot
        def velocity(z):
            sxx_r, sxy_l, sxz_l = col_state[0], col_state[1], col_state[2]
            sxx, sxy, sxz = stress[0, z], stress[1, z], stress[2, z]
            syz, szz, syy = stress[3, z], stress[4, z], stress[5, z]
            sxz_below = layer_state[1] if z == 0 else stress[2, z - 1]
            syz_below = layer_state[2] if z == 0 else stress[3, z - 1]
            szz_above = layer_state[0] if z == nz - 1 else stress[4, z + 1]
            scale = DT * buoy[z]
            vel[0, z] = vel[0, z] + scale * (
                ahead_x(sxx, col(sxx_r, 0, z)) - sxx + (sxy - behind_y(sxy)) + (sxz - sxz_below)
            )
            vel[1, z] = vel[1, z] + scale * (
                sxy - behind_x(sxy, col(sxy_l, 0, z)) + (ahead_y(syy) - syy) + (syz - syz_below)
            )
            vel[2, z] = vel[2, z] + scale * (
                sxz - behind_x(sxz, col(sxz_l, 0, z)) + (syz - behind_y(syz)) + (szz_above - szz)
            )

        for z in range(1, nz - 1):
            velocity(z)

        @pl.when(j > 0)
        def _():
            for kind in (2, 3, 6):
                finish(kind, other)
            vz_corner, vx_corner = got_rb[other], got_lt[other]
            at = 2 * GROUP + nz - 1
            col_state[0] = col_state[0] - DT * col_coef[0] * jnp.where(
                first_lane, vz_corner[:, at : at + 1], 0.0
            )
            col_state[2] = col_state[2] + DT * col_coef[2] * jnp.where(
                lane == nz - 1, vx_corner[:, :1], 0.0
            )
            layer_state[0] = layer_state[0] - DT * layer_coef[0] * jnp.where(
                first_lane, vx_corner[:, :1], 0.0
            )
            layer_state[1] = layer_state[1] + DT * layer_coef[2] * jnp.where(
                last_lane, vz_corner[:, at : at + 1], 0.0
            )

        velocity(0)
        velocity(nz - 1)

        rate = jnp.concatenate(
            [vel[0, z, y0 + 1 : y0 + 2] - vel[0, z, y0 : y0 + 1] for z in range(nz)], axis=0
        )
        fault = prestress[...] + FRIC * rate - got_acc[other, 0]

        for t in range(STEPS - 1):
            accs[slot, t] = got_acc[other, t + 1] + coefs[t] * rate
        accs[slot, STEPS - 1] = jnp.zeros((nz, nx), F32)

        heads, tails = [], []
        for z in range(nz):
            for c in range(3):
                f = vel[c, z]
                heads.append((c * GROUP + z, f[:, :1]))
                tails.append((c * GROUP + z, f[:, nx - 1 :]))
            tails.append((3 * GROUP + z, fault[z : z + 1, nx - 1 :]))
        own_first = pack(heads)
        own_last = pack(tails)
        pack0[slot] = own_first
        pack1[slot] = own_last
        start(1, slot)
        start(0, slot)
        start(4, slot)
        start(5, slot)

        @pl.when(j < STEPS - 1)
        def _():
            for kind in (2, 3, 6):
                start(kind, slot)

        def strain(z, low_z, top_x, top_y):
            vx, vy, vz = vel[0, z], vel[1, z], vel[2, z]
            vz_below = low_z if z == 0 else vel[2, z - 1]
            vx_above = top_x if z == nz - 1 else vel[0, z + 1]
            vy_above = top_y if z == nz - 1 else vel[1, z + 1]
            lam, mu = DT * lam_ref[z], DT * mu_ref[z]
            twice = 2.0 * mu
            strain_x = vx - behind_x(vx, 0.0)
            strain_y = vy - behind_y(vy)
            strain_z = vz - vz_below
            spread = lam * (strain_x + strain_y + strain_z)
            stress[0, z] = stress[0, z] + (twice * strain_x + spread)
            stress[5, z] = stress[5, z] + (twice * strain_y + spread)
            stress[4, z] = stress[4, z] + (twice * strain_z + spread)
            stress[1, z] = stress[1, z] + mu * (ahead_y(vx) - vx + (ahead_x(vy, 0.0) - vy))
            stress[2, z] = stress[2, z] + mu * (vx_above - vx + (ahead_x(vz, 0.0) - vz))
            stress[3, z] = stress[3, z] + mu * (vy_above - vy + (ahead_y(vz) - vz))

        for z in range(1, nz - 1):
            strain(z, None, None, None)
        finish(4, slot)
        finish(5, slot)
        top_x, top_y, top_z = got_t[slot, 0], got_t[slot, 1], got_t[slot, 2]
        low_x, low_y, low_z = got_b[slot, 0], got_b[slot, 1], got_b[slot, 2]
        strain(0, low_z, top_x, top_y)
        strain(nz - 1, low_z, top_x, top_y)

        finish(0, slot)
        finish(1, slot)
        column_r, column_l = got_r[slot], got_l[slot]
        for z in range(nz):
            lam, mu = DT * lam_ref[z], DT * mu_ref[z]
            behind = jnp.where(first_lane, -col(column_l, 0, z), 0.0)
            spread = lam * behind
            stress[0, z] = stress[0, z] + (2.0 * mu * behind + spread)
            stress[5, z] = stress[5, z] + spread
            stress[4, z] = stress[4, z] + spread
            sxy = stress[1, z] + mu * jnp.where(last_lane, col(column_r, 1, z), 0.0)
            stress[1, z] = sxy
            stress[1, z, y0 : y0 + 1] = jnp.where(
                mask[z : z + 1] == 1, fault[z : z + 1], sxy[y0 : y0 + 1]
            )
            stress[2, z] = stress[2, z] + mu * jnp.where(
                last_lane, col(column_r, 2, z), 0.0
            )

        got_first, got_last = column_r, column_l

        lam_r, mu_r, mu_l = col_coef[0], col_coef[1], col_coef[2]
        strain_x = got_first - own_last
        strain_y = lanes_down(got_first - behind_y(got_first), GROUP)
        strain_z = lanes_down(got_first - pltpu.roll(got_first, 1, 1), 2 * GROUP)
        col_state[0] = col_state[0] + DT * (
            (lam_r + 2.0 * mu_r) * strain_x + lam_r * (strain_y + strain_z)
        )
        jump = own_first - got_last
        sheared = col_state[1] + DT * mu_l * (ahead_y(got_last) - got_last + lanes_down(jump, GROUP))
        col_state[1] = jnp.where(
            jnp.logical_and(row == y0, col_coef[3] > 0.5),
            lanes_down(got_last, 3 * GROUP),
            sheared,
        )
        col_state[2] = col_state[2] + DT * mu_l * (
            lanes_down(got_last, 1) - got_last + lanes_down(jump, 2 * GROUP)
        )

        lam_t, mu_t = layer_coef[0], layer_coef[1]
        layer_state[0] = layer_state[0] + DT * (
            (lam_t + 2.0 * mu_t) * (top_z - vel[2, nz - 1])
            + lam_t * (top_x - behind_x(top_x, 0.0) + (top_y - behind_y(top_y)))
        )
        low_mu = DT * layer_coef[2]
        layer_state[1] = layer_state[1] + low_mu * (
            vel[0, 0] - low_x + (ahead_x(low_z, 0.0) - low_z)
        )
        layer_state[2] = layer_state[2] + low_mu * (
            vel[1, 0] - low_y + (ahead_y(low_z) - low_z)
        )
        return carry

    lax.fori_loop(0, STEPS, step, 0)


def per_device(n_strike, n_depth, *args):
    nz, ny, nx = args[2].shape
    slab = (2, ny, nx)
    vmem = pl.BlockSpec(memory_space=pltpu.VMEM)
    specs = [pl.BlockSpec(memory_space=pl.ANY)] * len(args)
    specs[6] = pl.BlockSpec(memory_space=pltpu.SMEM)
    return pl.pallas_call(
        functools.partial(kernel, n_strike, n_depth),
        out_shape=tuple(jax.ShapeDtypeStruct(a.shape, a.dtype) for a in args[:2]),
        in_specs=specs,
        out_specs=(vmem, vmem),
        scratch_shapes=[
            *(pltpu.VMEM(args[i].shape, args[i].dtype) for i in (2, 3, 4, 5, 7, 8)),
            pltpu.VMEM(slab, F32),
            pltpu.VMEM(slab, F32),
            pltpu.VMEM((2, STEPS, nz, nx), F32),
            pltpu.VMEM((2, 3, ny, nx), F32),
            pltpu.VMEM(slab, F32),
            pltpu.VMEM(slab, F32),
            pltpu.VMEM(slab, F32),
            pltpu.VMEM(slab, F32),
            pltpu.VMEM((2, 3, ny, nx), F32),
            pltpu.VMEM((2, 3, ny, nx), F32),
            pltpu.VMEM((2, STEPS, nz, nx), F32),
            pltpu.VMEM((3, ny, nx), F32),
            pltpu.VMEM((4, ny, nx), F32),
            pltpu.VMEM((3, ny, nx), F32),
            pltpu.VMEM((3, ny, nx), F32),
            pltpu.SemaphoreType.DMA((7, 2)),
            pltpu.SemaphoreType.DMA((7, 2)),
            pltpu.SemaphoreType.DMA((8,)),
        ],
        compiler_params=pltpu.CompilerParams(collective_id=0, has_side_effects=True),
    )(*args)


def solution(mesh):
    wide = P(None, "depth", None, "strike")
    placed = (
        wide,
        wide,
        P("depth", None, "strike"),
        P("depth", None, "strike"),
        P("depth", None, "strike"),
        P(None, "depth", "strike"),
        P(),
        P("depth", "strike"),
        P("depth", "strike"),
    )
    return jax.shard_map(
        functools.partial(per_device, mesh.shape["strike"], mesh.shape["depth"]),
        mesh=mesh,
        in_specs=placed,
        out_specs=(wide, wide),
        check_vma=False,
    )
```
